32 devices in a mesh: row: 8 (over y, x, core), col: 4 (over z).
Axes of the slice: x: 2, y: 2, z: 4, core: 2. Of those that a mesh axis runs over, the one named last changes fastest.
Arguments:
- ancestor: float32 [9, 9, 512, 512], P(None, None, 'row', 'col'), may hold values from -1 to 4, as said below
- inverse_first: float32 [2, 2, 512, 512], P(None, None, 'row', 'col'), may hold values from -1 to 2, as said below
- panel_first: float32 [1536, 2, 512], P('row', None, 'col'), may hold values from -0.15625 to 0.15625
- structure_first: int32 [1536], replicated, may hold values from 0 to 4607, as said below
- inverse_second: float32 [1, 1, 512, 512], P(None, None, 'row', 'col'), may hold values from -1 to 2, as said below
- panel_second: float32 [1536, 1, 512], P('row', None, 'col'), may hold values from -0.15625 to 0.15625
- structure_second: int32 [1536], replicated, may hold values from 0 to 5631, as said below
Outputs:
- row_first: float32 [2, 11, 512, 512], P(None, None, 'row', 'col')
- row_second: float32 [1, 12, 512, 512], P(None, None, 'row', 'col')
The draws below stay inside these ranges and needn't reach their ends.
Inputs may be any that keep to these rules, and one draw needn't show every extreme that they name: `ancestor`: symmetric and positive definite as a matrix. `inverse_first`: symmetric and positive definite as a matrix. `inverse_second`: symmetric and positive definite as a matrix. `structure_first`: entries are distinct; every aligned group of 16 ancestor rows holds at most 6 entries, and some group holds exactly 6. `structure_second`: entries are distinct; every aligned group of 16 ancestor rows holds at most 6 entries, and some group holds exactly 6.
All inputs are finite; a program needn't handle non-finite values.
Results may differ from the reference program's by a relative error of at most 0.000075.
Values sent between devices are 32-bit elements; how exact they have to be, the bound alone decides.
A program may use at most 128 MiB of HBM per device.

```python
import jax
import jax.numpy as jnp
from jax import lax

ANC = 4608
WA = 1024
WB = 512
NSA = 1536
NSB = 1536
TILE = 512
GRAIN = 16
CAP = 6
RH = 64
CW = 128


def pack_tiles(tiled):
    first, second = (tiled.shape[0], tiled.shape[1])
    grid_rows = TILE // RH
    grid_cols = TILE // CW
    depth = RH * CW // 128
    blocks = tiled.reshape(first, second, grid_rows, RH, grid_cols, CW).transpose(0, 1, 2, 4, 3, 5)
    blocks = blocks.reshape(first, second, grid_rows, grid_cols, depth, 128).transpose(0, 1, 2, 4, 3, 5)
    return blocks.reshape(first, second, grid_rows * depth, grid_cols * 128)


def definite_tiles(key, row_count, floor_level, ceiling_level, spread):
    first, second = jax.random.split(key)
    noise_field = jax.random.normal(first, (row_count, row_count), jnp.float32)
    levels = jax.random.uniform(second, (row_count,), jnp.float32, floor_level, ceiling_level)
    symmetric = (noise_field + noise_field.T) * (spread / jnp.sqrt(2.0 * row_count))
    matrix = symmetric + jnp.diag(levels)
    tile_count = row_count // TILE
    return pack_tiles(matrix.reshape(tile_count, TILE, tile_count, TILE).transpose(0, 2, 1, 3))


def grouped_structure(key, row_count, entry_count):
    group_count = row_count // GRAIN
    slot_count = group_count * CAP
    first_key, second_key, third_key = jax.random.split(key, 3)
    shuffled = jax.random.permutation(first_key, slot_count).astype(jnp.int32)
    forced = jax.random.randint(second_key, (), 0, group_count).astype(jnp.int32)
    slot_group = jnp.arange(slot_count, dtype=jnp.int32) // CAP
    ranking = jnp.where(slot_group == forced, shuffled - slot_count, shuffled)
    chosen = jnp.argsort(ranking, stable=True)[:entry_count].astype(jnp.int32)
    group_keys = jax.random.split(third_key, group_count)
    offsets = jax.vmap(lambda single: jax.random.permutation(single, GRAIN)[:CAP].astype(jnp.int32))(group_keys)
    group_of = chosen // CAP
    row_ids = group_of * GRAIN + offsets[group_of, chosen % CAP]
    return row_ids.astype(jnp.int32)


def draw_ancestor(key, part):
    return definite_tiles(jax.random.fold_in(key, 11), ANC, 1.5, 3.0, 0.7)


def draw_inverse_first(key, part):
    return definite_tiles(jax.random.fold_in(key, 12), WA, 0.8, 1.5, 0.3)


def draw_inverse_second(key, part):
    return definite_tiles(jax.random.fold_in(key, 13), WB, 0.8, 1.5, 0.3)


def draw_structure_first(key, part):
    return grouped_structure(jax.random.fold_in(key, 21), ANC, NSA)


def draw_structure_second(key, part):
    return grouped_structure(jax.random.fold_in(key, 22), ANC + WA, NSB)


def shard_levels(own_key, shape, cuts, low, high):
    level = 1.0
    for dim, parts in cuts:
        steps = jax.random.uniform(jax.random.fold_in(jax.random.fold_in(own_key, 6), dim), (parts,), jnp.float32, low / len(cuts), high / len(cuts))
        level = level * jnp.repeat(jnp.exp(steps), shape[dim] // parts).reshape((-1,) + (1,) * (len(shape) - 1 - dim))
    return level


def gaussian(rng, dims, scale, limit, shards=(), held_as=jnp.bfloat16):
    array = scale * jax.random.normal(rng, dims, jnp.float32)
    if shards:
        array = array * shard_levels(rng, dims, shards, -0.22, 0.18)
    return jnp.clip(array, -limit, limit).astype(held_as)


def setup_inputs(seed: int = 0) -> dict:
    arg_keys = jax.random.split(jax.random.key(seed), 8)
    return {
        "ancestor": draw_ancestor(jax.random.fold_in(arg_keys[7], 71), 0),
        "inverse_first": draw_inverse_first(jax.random.fold_in(arg_keys[7], 71), 0),
        "panel_first": gaussian(arg_keys[2], (NSA, WA // TILE, TILE), NSA ** -0.5, 0.15625, ((0, 8), (2, 4)), jnp.float32),
        "structure_first": draw_structure_first(jax.random.fold_in(arg_keys[7], 71), 0),
        "inverse_second": draw_inverse_second(jax.random.fold_in(arg_keys[7], 71), 0),
        "panel_second": gaussian(arg_keys[5], (NSB, WB // TILE, TILE), NSB ** -0.5, 0.15625, ((0, 8), (2, 4)), jnp.float32),
        "structure_second": draw_structure_second(jax.random.fold_in(arg_keys[7], 71), 0),
    }


def unpack(packed):
    first, second = packed.shape[0], packed.shape[1]
    grid_rows = TILE // RH
    grid_cols = TILE // CW
    depth = RH * CW // 128
    blocks = packed.reshape(first, second, grid_rows, depth, grid_cols, 128).transpose(0, 1, 2, 4, 3, 5)
    blocks = blocks.reshape(first, second, grid_rows, grid_cols, RH, CW).transpose(0, 1, 2, 4, 3, 5)
    return blocks.reshape(first, second, TILE, TILE)


def pack(tiled):
    first, second = tiled.shape[0], tiled.shape[1]
    grid_rows = TILE // RH
    grid_cols = TILE // CW
    depth = RH * CW // 128
    blocks = tiled.reshape(first, second, grid_rows, RH, grid_cols, CW).transpose(0, 1, 2, 4, 3, 5)
    blocks = blocks.reshape(first, second, grid_rows, grid_cols, depth, 128).transpose(0, 1, 2, 4, 3, 5)
    return blocks.reshape(first, second, grid_rows * depth, grid_cols * 128)


def from_tiles(packed):
    tiled = unpack(packed)
    first, second, height, width = tiled.shape
    return tiled.transpose(0, 2, 1, 3).reshape(first * height, second * width)


def to_tiles(matrix):
    first = matrix.shape[0] // TILE
    second = matrix.shape[1] // TILE
    return pack(matrix.reshape(first, TILE, second, TILE).transpose(0, 2, 1, 3))


def sweep_step(frontier, inverse, panel_part, structure):
    flattened = panel_part.reshape(panel_part.shape[0], -1)
    spread = jnp.zeros((frontier.shape[0], flattened.shape[1]), jnp.float32).at[structure].set(flattened)
    image = jnp.dot(frontier, spread, precision=lax.Precision.HIGHEST, preferred_element_type=jnp.float32)
    diagonal = from_tiles(inverse) + jnp.dot(spread.T, image, precision=lax.Precision.HIGHEST, preferred_element_type=jnp.float32)
    row_block = jnp.concatenate([-image.T, diagonal], axis=1)
    upper_rows = jnp.concatenate([frontier, -image], axis=1)
    grown = jnp.concatenate([upper_rows, row_block], axis=0)
    return row_block, grown


def reference(ancestor, inverse_first, panel_first, structure_first, inverse_second, panel_second, structure_second):
    first_block, frontier = sweep_step(from_tiles(ancestor), inverse_first, panel_first, structure_first)
    second_block, unused = sweep_step(frontier, inverse_second, panel_second, structure_second)
    return to_tiles(first_block), to_tiles(second_block)
```

```python
import jax
import jax.numpy as jnp
from jax import lax
from jax.sharding import PartitionSpec as P

TILE = 512
GRAIN = 16
CAP = 6


def open_packed(packed, row_height, col_width):
    return packed.reshape(packed.shape[0], packed.shape[1], row_height, col_width)


def close_packed(tiles):
    depth = tiles.shape[2] * tiles.shape[3] // 128
    return tiles.reshape(tiles.shape[0], tiles.shape[1], depth, 128)


def product(left, right, left_dim=1):
    return lax.dot_general(
        left,
        right,
        (((left_dim,), (0,)), ((), ())),
        precision=lax.Precision.HIGH,
        preferred_element_type=jnp.float32,
    )


def entry_ranks(structure):
    group = structure // GRAIN
    order = jnp.arange(structure.shape[0], dtype=jnp.int32)
    same = (group[:, None] == group[None, :]) & (order[None, :] < order[:, None])
    return jnp.sum(same.astype(jnp.int32), axis=1)


def slots_within(structure, ranks, height):
    owner = structure % TILE // height
    group = structure // TILE * (height // GRAIN) + structure % height // GRAIN
    return owner, group * CAP + ranks


def one_hot(marks, count):
    return (jnp.arange(count, dtype=jnp.int32)[:, None] == marks[None, :]).astype(jnp.float32)


def local_rows(structure, marks, count, height):
    row = structure // TILE * height + structure % height
    match = jnp.arange(count, dtype=jnp.int32)[:, None] == marks[None, :]
    return jnp.max(jnp.where(match, row[None, :], -1), axis=1)


def on_device(
    ancestor,
    inverse_first,
    panel_first,
    structure_first,
    inverse_second,
    panel_second,
    structure_second,
):
    rows = lax.axis_size("row")
    cols = lax.axis_size("col")
    height = TILE // rows
    width = TILE // cols
    halves = width // height
    row_index = lax.axis_index("row")
    col_index = lax.axis_index("col")
    blocks = open_packed(ancestor, height, width)
    first_diag = open_packed(inverse_first, height, width)
    second_diag = open_packed(inverse_second, height, width)
    tiles = blocks.shape[0]
    first = first_diag.shape[0]
    second = second_diag.shape[0]
    every = first + second
    limit = tiles * TILE
    first_width = first * width

    panels = jnp.concatenate(
        [panel_first.reshape(-1, first_width), panel_second.reshape(-1, second * width)], axis=1
    )
    both = lax.all_gather(panels, "row", axis=0, tiled=True)
    whole_first = both[:, :first_width]
    whole_second = both[:, first_width:]

    above = structure_second < limit
    ranks_first = entry_ranks(structure_first)
    ranks_second = entry_ranks(structure_second)
    row_slots = tiles * height // GRAIN * CAP
    col_slots = tiles * width // GRAIN * CAP
    low_slots = first * TILE // GRAIN * CAP
    owner, slot = slots_within(structure_first, ranks_first, height)
    row_marks_first = jnp.where(owner == row_index, slot, -1)
    owner, slot = slots_within(structure_second, ranks_second, height)
    row_marks_second = jnp.where(above & (owner == row_index), slot, -1)
    owner, slot = slots_within(structure_first, ranks_first, width)
    all_marks_first = owner * col_slots + slot
    col_marks_first = jnp.where(owner == col_index, slot, -1)
    owner, slot = slots_within(structure_second, ranks_second, width)
    all_marks_second = jnp.where(above, owner * col_slots + slot, -1)
    col_marks_second = jnp.where(above & (owner == col_index), slot, -1)
    below = structure_second - limit
    low_marks = jnp.where(above, -1, below // GRAIN * CAP + ranks_second)
    low_match = jnp.arange(low_slots, dtype=jnp.int32)[:, None] == low_marks[None, :]
    low_rows = jnp.max(jnp.where(low_match, below[None, :], -1), axis=1)

    take_first = one_hot(row_marks_first, row_slots)
    take_second = one_hot(
        jnp.where(above, row_marks_second, row_slots + low_marks), row_slots + low_slots
    )
    part_first = product(take_first, whole_first)
    part_second = product(take_second, whole_second)
    part_first = part_first.reshape(row_slots, first, halves, height).transpose(0, 2, 1, 3)
    part_first = part_first.reshape(row_slots * first, width)
    part_second = part_second.reshape(row_slots + low_slots, second, halves, height)
    part_second = part_second.transpose(0, 2, 1, 3)
    part_second = part_second.reshape((row_slots + low_slots) * second, width)
    spread = lax.all_gather(jnp.concatenate([part_first, part_second], axis=0), "col", axis=0)
    cut = part_first.shape[0]
    got_first = spread[:, :cut].reshape(cols, row_slots, halves, first, height)
    got_second = spread[:, cut:].reshape(cols, row_slots + low_slots, halves, second, height)
    got_first = got_first.transpose(1, 0, 2, 3, 4).reshape(row_slots, rows, first * height)
    got_second = got_second.transpose(1, 0, 2, 3, 4).reshape(-1, rows, second * height)
    upper_second = got_second[:row_slots]
    low_second = got_second[row_slots:].reshape(low_slots, second * TILE)

    flat = blocks.transpose(0, 2, 1, 3).reshape(tiles * height, tiles * width)
    kept_rows = jnp.concatenate(
        [
            local_rows(structure_first, row_marks_first, row_slots, height),
            local_rows(structure_second, row_marks_second, row_slots, height),
        ]
    )
    take_kept = (
        kept_rows[:, None] == jnp.arange(tiles * height, dtype=jnp.int32)[None, :]
    ).astype(jnp.float32)
    kept = product(take_kept, flat)

    place = jnp.arange(first * TILE, dtype=jnp.int32)
    place_row = place // (first * height)
    place_tile = place // height % first
    named = place_tile * TILE + place_row * height + place % height
    meet_low = (named[:, None] == low_rows[None, :]).astype(jnp.float32)
    first_at_low = product(got_first.reshape(row_slots, first * TILE), meet_low)
    folded = product(first_at_low, low_second).reshape(row_slots, rows, second * height)
    left = jnp.concatenate(
        [
            jnp.concatenate([got_first, -folded], axis=2),
            jnp.concatenate(
                [jnp.zeros((row_slots, rows, first * height), jnp.float32), upper_second], axis=2
            ),
        ],
        axis=0,
    )
    partial = product(left.reshape(2 * row_slots, every * TILE), kept, 0)
    partial = partial.reshape(rows, every * height, tiles * width)

    own_low = jnp.arange(first * height, dtype=jnp.int32)
    own_low = own_low // height * TILE + row_index * height + own_low % height
    own_meet = (own_low[:, None] == low_rows[None, :]).astype(jnp.float32)
    own_second = product(own_meet, low_second)
    flat_diag = first_diag.transpose(0, 2, 1, 3).reshape(first * height, first_width)
    low_partial = product(own_second, flat_diag, 0)
    low_partial = low_partial.reshape(rows, second * height, first_width)

    slabs = [low_partial[:, :, k * width : (k + 1) * width] for k in range(first)]
    slabs.append(jnp.zeros((rows, (every - first * second) * height, width), jnp.float32))
    joined = jnp.concatenate([partial, jnp.concatenate(slabs, axis=1)], axis=2)
    summed = lax.psum_scatter(joined, "row", scatter_dimension=0, tiled=False)
    image = summed[:, : tiles * width]
    step = second * height
    low_image = jnp.concatenate(
        [summed[k * step : (k + 1) * step, tiles * width :] for k in range(first)], axis=1
    )

    edge = first * height
    column_ids = jnp.arange(tiles * width, dtype=jnp.int32)
    col_rows_first = local_rows(structure_first, col_marks_first, col_slots, width)
    col_rows_second = local_rows(structure_second, col_marks_second, col_slots, width)
    pick_first = (column_ids[:, None] == col_rows_first[None, :]).astype(jnp.float32)
    pick_second = (column_ids[:, None] == col_rows_second[None, :]).astype(jnp.float32)
    picked = jnp.concatenate([product(image, pick_first), product(image[edge:], pick_second)], axis=0)
    met = lax.all_gather(picked, "col", axis=0)
    met = met.transpose(1, 0, 2).reshape(-1, cols * col_slots)
    dense_first = product(one_hot(all_marks_first, cols * col_slots), whole_first)
    dense_second = product(one_hot(all_marks_second, cols * col_slots), whole_second)
    corner = product(met[: every * height], dense_first)
    low_block = low_image - corner[edge:]
    low_all = lax.all_gather(low_block, "col", axis=0)
    low_all = low_all.transpose(1, 0, 2).reshape(second * height, first * TILE)
    spot = jnp.arange(first * TILE, dtype=jnp.int32)
    spot = spot // width % first * TILE + spot // first_width * width + spot % width
    below_marks = jnp.where(above, -1, below)
    dense_low = product(
        (spot[:, None] == below_marks[None, :]).astype(jnp.float32), whole_second
    )
    final = product(met[every * height :], dense_second) + product(low_all, dense_low)

    def tiled(matrix, up, across):
        return matrix.reshape(up, height, across, width).transpose(0, 2, 1, 3)

    row_first = jnp.concatenate(
        [-tiled(image[:edge], first, tiles), first_diag + tiled(corner[:edge], first, first)], axis=1
    )
    row_second = jnp.concatenate(
        [
            -tiled(image[edge:], second, tiles),
            -tiled(low_block, second, first),
            second_diag + tiled(final, second, second),
        ],
        axis=1,
    )
    return (close_packed(row_first), close_packed(row_second))


def solution(mesh):
    in_specs = (
        P(None, None, "row", "col"),
        P(None, None, "row", "col"),
        P("row", None, "col"),
        P(),
        P(None, None, "row", "col"),
        P("row", None, "col"),
        P(),
    )
    out_specs = (P(None, None, "row", "col"), P(None, None, "row", "col"))
    return jax.shard_map(
        on_device, mesh=mesh, in_specs=in_specs, out_specs=out_specs, check_vma=False
    )
```
